32 devices in a mesh: grp: 2 (over x), own: 8 (over z, y), shot: 2 (over core).
Axes of the slice: x: 2, y: 2, z: 4, core: 2. Of those that a mesh axis runs over, the one named last changes fastest.
Arguments:
- velocity: bfloat16 [2048, 4, 4, 128], P(('grp', 'own')), parts along dimension 0, may hold values from 1.5 to 4.5
- density: bfloat16 [2048, 4, 4, 128], P(('grp', 'own')), parts along dimension 0, may hold values from 1 to 2.59375
- tile_home: int32 [2048], P('grp'), parts along dimension 0, may hold values from 0 to 1023, as said below
- footprints: int32 [16, 2, 2, 64], P('grp'), parts along dimension 0, may hold values from 0 to 1023, as said below
- source_cell: int32 [16, 2, 2], P(('grp', 'own'), 'shot'), parts along dimension 0, may hold values from 0 to 131071
- source_wave: float32 [16, 2, 2, 2], P(('grp', 'own'), 'shot'), parts along dimension 0, may hold values from -16 to 16
- receivers: int32 [16, 2, 2, 128], P(('grp', 'own'), 'shot'), parts along dimension 0, may hold values from 0 to 131071
- observed: float32 [16, 2, 2, 2, 128], P(('grp', 'own'), 'shot'), parts along dimension 0, may hold values from -6 to 6
- pressure_old: bfloat16 [16, 2, 2, 32, 32, 128], P(('grp', 'own'), 'shot'), parts along dimension 0, may hold values from -6 to 6
- pressure_now: bfloat16 [16, 2, 2, 32, 32, 128], P(('grp', 'own'), 'shot'), parts along dimension 0, may hold values from -6 to 6
- adjoint_next: bfloat16 [16, 2, 2, 32, 32, 128], P(('grp', 'own'), 'shot'), parts along dimension 0, may hold values from -6 to 6
- adjoint_now: bfloat16 [16, 2, 2, 32, 32, 128], P(('grp', 'own'), 'shot'), parts along dimension 0, may hold values from -6 to 6
Outputs:
- velocity_gradient: float32 [2048, 4, 4, 128], P(('grp', 'own'), 'shot'), parts along dimension 0
The draws below stay inside these ranges and needn't reach their ends.
There are 2 independent parts, one for each index of `grp`. The reference program is written for one: setup_inputs(seed, part) draws one part's arguments, and reference() takes and returns one part's arrays. A program takes and returns all parts, laid end to end along the dimension named above; each array names one. Nothing has to cross between parts.
Inputs may be any that keep to these rules, and one draw needn't show every extreme that they name: `tile_home`: a permutation of the rows; a row's owner is row // 128; with tiles numbered row by row over the 32 x 32 grid, every square block of 8 x 8 tiles holds exactly 8 tiles of each owner. `footprints`: each list names the tiles of one square block of 8 x 8 tiles of the grid, row by row.
All inputs are finite; a program needn't handle non-finite values.
Results may differ from the reference program's by a relative error of at most 0.0003.
Values may be sent and summed in bfloat16 or wider, within the bound.
A program may use at most 64 MiB of HBM per device.

```python
import jax
import jax.numpy as jnp
from jax import lax

TX = 4
TY = 4
NZ = 128
GT = 32
FT = 8
SHOTS_DEV = 2
NREC = 128
NTILE = 1024
TPO = 128
FX = 32
FY = 32
CELLS = 131072
N_OWN = 8
N_SHOT = 2


def draw_tile_home(key, part):
    owners = GT * GT // TPO
    exponent = owners.bit_length() - 1
    across = 2 ** ((exponent + 1) // 2)
    along = owners // across
    key_owner, key_local = jax.random.split(jax.random.fold_in(key, 17))
    owner_order = jax.random.permutation(key_owner, owners)
    local_order = jax.random.permutation(key_local, TPO)
    tile_x = jnp.arange(GT)[:, None]
    tile_y = jnp.arange(GT)[None, :]
    owner_of = owner_order[tile_x % across * along + tile_y % along]
    local_of = local_order[tile_x // across * (GT // along) + tile_y // along]
    return (owner_of * TPO + local_of).reshape(-1).astype(jnp.int32)


def draw_footprints(key, part):
    shot_total = N_OWN * N_SHOT * SHOTS_DEV
    key_x, key_y = jax.random.split(jax.random.fold_in(key, 23))
    anchor_x = jax.random.randint(key_x, (shot_total,), 0, GT - FT + 1)
    anchor_y = jax.random.randint(key_y, (shot_total,), 0, GT - FT + 1)
    anchor_x = anchor_x.at[0].set(GT - FT).at[1].set(0)
    anchor_y = anchor_y.at[0].set(GT - FT).at[1].set(0)
    position = jnp.arange(FT * FT)
    tile_lists = (anchor_x[:, None] + position[None, :] // FT) * GT + anchor_y[:, None] + position[None, :] % FT
    return tile_lists.reshape(N_OWN, N_SHOT, SHOTS_DEV, FT * FT).astype(jnp.int32)


def set_ends(entries, key, least, largest):
    longest = entries.shape.index(max(entries.shape))
    spots = []
    for shift in (0, 1):
        where = [jax.random.randint(jax.random.fold_in(key, axis), (), 0, length) for axis, length in enumerate(entries.shape)]
        where[longest] = (where[longest] + shift) % entries.shape[longest]
        spots.append(tuple(where))
    return entries.at[spots[0]].set(least).at[spots[1]].set(largest)


def block_levels(stream_key, extent, cuts, smallest, top_value):
    def one(dim, blocks):
        heights = jax.random.uniform(jax.random.fold_in(jax.random.fold_in(stream_key, 6), dim), (blocks,), jnp.float32, smallest / len(cuts), top_value / len(cuts))
        return jnp.repeat(jnp.exp(heights), extent[dim] // blocks).reshape((-1,) + (1,) * (len(extent) - dim - 1))

    factor_of = one(*cuts[0])
    for cut in cuts[1:]:
        factor_of = factor_of * one(*cut)
    return factor_of


def noise(own_key, extent, scale, most, cuts=(), kind=jnp.bfloat16):
    drawn = scale * jax.random.normal(own_key, extent, jnp.float32)
    if cuts:
        drawn = drawn * block_levels(own_key, extent, cuts, -0.22, 0.18)
    return jnp.clip(drawn, -most, most).astype(kind)


def setup_inputs(seed: int = 0, part: int = 0) -> dict:
    key_list = jax.random.split(jax.random.key(seed), 13)
    part_keys = jax.random.split(jax.random.fold_in(key_list[12], part), 13)
    return {
        "velocity": jnp.clip(1.5 + 3.0 * jax.random.uniform(part_keys[0], (NTILE, TX, TY, NZ), jnp.float32) ** block_levels(part_keys[0], (NTILE, TX, TY, NZ), ((0, 8),), -0.2, 0.2), 1.5, 4.5).astype(jnp.bfloat16),
        "density": jnp.clip(1.0 + 1.59375 * jax.random.uniform(part_keys[1], (NTILE, TX, TY, NZ), jnp.float32) ** block_levels(part_keys[1], (NTILE, TX, TY, NZ), ((0, 8),), -0.2, 0.2), 1.0, 2.59375).astype(jnp.bfloat16),
        "tile_home": draw_tile_home(jax.random.fold_in(jax.random.fold_in(key_list[12], part), 71), part),
        "footprints": draw_footprints(jax.random.fold_in(jax.random.fold_in(key_list[12], part), 71), part),
        "source_cell": set_ends(jax.random.randint(part_keys[4], (N_OWN, N_SHOT, SHOTS_DEV), 0, CELLS), jax.random.fold_in(part_keys[4], 1), 0, CELLS - 1).astype(jnp.int32),
        "source_wave": noise(part_keys[5], (N_OWN, N_SHOT, SHOTS_DEV, 2), 4.0, 16.0, ((0, 8), (1, 2)), jnp.float32),
        "receivers": set_ends(jax.random.randint(part_keys[6], (N_OWN, N_SHOT, SHOTS_DEV, NREC), 0, CELLS), jax.random.fold_in(part_keys[6], 1), 0, CELLS - 1).astype(jnp.int32),
        "observed": noise(part_keys[7], (N_OWN, N_SHOT, SHOTS_DEV, 2, NREC), 1.0, 6.0, ((0, 8), (1, 2)), jnp.float32),
        "pressure_old": noise(part_keys[8], (N_OWN, N_SHOT, SHOTS_DEV, FX, FY, NZ), 1.0, 6.0, ((0, 8), (1, 2))),
        "pressure_now": noise(part_keys[9], (N_OWN, N_SHOT, SHOTS_DEV, FX, FY, NZ), 1.0, 6.0, ((0, 8), (1, 2))),
        "adjoint_next": noise(part_keys[10], (N_OWN, N_SHOT, SHOTS_DEV, FX, FY, NZ), 1.0, 6.0, ((0, 8), (1, 2))),
        "adjoint_now": noise(part_keys[11], (N_OWN, N_SHOT, SHOTS_DEV, FX, FY, NZ), 1.0, 6.0, ((0, 8), (1, 2))),
    }


STENCIL = (1225.0 / 1024.0, -245.0 / 3072.0, 49.0 / 5120.0, -5.0 / 7168.0)
COURANT = 0.09


def take_cells(wavefield, dimension, first_cell, length):
    return lax.slice_in_dim(wavefield, first_cell, first_cell + length, axis=dimension)


def half_buoyancy(buoyancy, dimension):
    length = buoyancy.shape[dimension]
    following = jnp.concatenate([take_cells(buoyancy, dimension, 1, length - 1), take_cells(buoyancy, dimension, length - 1, 1)], axis=dimension)
    return 0.5 * (buoyancy + following)


def pad_along(wavefield, dimension):
    widths = [(4, 4) if index_dim == dimension else (0, 0) for index_dim in range(3)]
    return jnp.pad(wavefield, widths)


def apply_operator(wavefield, half_buoys):
    summed = jnp.zeros_like(wavefield)
    for dimension in range(3):
        length = wavefield.shape[dimension]
        padded = pad_along(wavefield, dimension)
        gradient = jnp.zeros_like(wavefield)
        for position, weight in enumerate(STENCIL):
            distance = position + 1
            gradient = gradient + weight * (take_cells(padded, dimension, 4 + distance, length) - take_cells(padded, dimension, 5 - distance, length))
        flux_pad = pad_along(half_buoys[dimension] * gradient, dimension)
        for position, weight in enumerate(STENCIL):
            distance = position + 1
            summed = summed + weight * (take_cells(flux_pad, dimension, 3 + distance, length) - take_cells(flux_pad, dimension, 4 - distance, length))
    return summed


def inject(wavefield, cell_index, amounts):
    return wavefield.reshape(-1).at[cell_index].add(amounts).reshape(wavefield.shape)


def record(wavefield, cell_index):
    return wavefield.reshape(-1)[cell_index]


def run_shot(velocity, density, pressure_old, pressure_now, adjoint_next, adjoint_now, source_cell, source_wave, receivers, observed):
    coupling = (COURANT * velocity) ** 2 * density
    buoyancy = 1.0 / density
    half_buoys = tuple(half_buoyancy(buoyancy, dimension) for dimension in range(3))
    image_one = apply_operator(pressure_now, half_buoys)
    pressure_two = inject(2.0 * pressure_now - pressure_old + coupling * image_one, source_cell, source_wave[0])
    image_two = apply_operator(pressure_two, half_buoys)
    pressure_three = inject(2.0 * pressure_two - pressure_now + coupling * image_two, source_cell, source_wave[1])
    misfit_one = record(pressure_two, receivers) - observed[0]
    misfit_two = record(pressure_three, receivers) - observed[1]
    adjoint_one = inject(2.0 * adjoint_now - adjoint_next + coupling * apply_operator(adjoint_now, half_buoys), receivers, misfit_two)
    adjoint_zero = inject(2.0 * adjoint_one - adjoint_now + coupling * apply_operator(adjoint_one, half_buoys), receivers, misfit_one)
    return 2.0 * COURANT * COURANT * velocity * density * (adjoint_one * image_two + adjoint_zero * image_one)


def tiles_to_field(tiles, per_side):
    tile_x, tile_y, depth = tiles.shape[1], tiles.shape[2], tiles.shape[3]
    grid = tiles.reshape(per_side, per_side, tile_x, tile_y, depth).transpose(0, 2, 1, 3, 4)
    return grid.reshape(per_side * tile_x, per_side * tile_y, depth)


def field_to_tiles(wavefield, per_side):
    tile_x = wavefield.shape[0] // per_side
    tile_y = wavefield.shape[1] // per_side
    depth = wavefield.shape[2]
    grid = wavefield.reshape(per_side, tile_x, per_side, tile_y, depth).transpose(0, 2, 1, 3, 4)
    return grid.reshape(per_side * per_side, tile_x, tile_y, depth)


def reference(velocity, density, tile_home, footprints, source_cell, source_wave, receivers, observed, pressure_old, pressure_now, adjoint_next, adjoint_now):
    shot_total = N_OWN * N_SHOT * SHOTS_DEV
    field_shape = (shot_total, FT * TX, FT * TY, NZ)
    inputs = (footprints.reshape(shot_total, FT * FT), source_cell.reshape(shot_total), source_wave.reshape(shot_total, 2), receivers.reshape(shot_total, NREC), observed.reshape(shot_total, 2, NREC), pressure_old.reshape(field_shape), pressure_now.reshape(field_shape), adjoint_next.reshape(field_shape), adjoint_now.reshape(field_shape))

    def accumulate(gradient_sum, shot_inputs):
        tile_list, cell_one, wave_one, receiver_list, observed_one, field_old, field_now, field_next, field_adj = shot_inputs
        home_rows = tile_home[tile_list]
        shot_velocity = tiles_to_field(velocity[home_rows], FT).astype(jnp.float32)
        shot_density = tiles_to_field(density[home_rows], FT).astype(jnp.float32)
        shot_gradient = run_shot(shot_velocity, shot_density, field_old.astype(jnp.float32), field_now.astype(jnp.float32), field_next.astype(jnp.float32), field_adj.astype(jnp.float32), cell_one, wave_one, receiver_list, observed_one)
        return gradient_sum.at[home_rows].add(field_to_tiles(shot_gradient, FT)), None

    initial = jnp.zeros((GT * GT, TX, TY, NZ), jnp.float32)
    velocity_gradient, unused = lax.scan(accumulate, initial, inputs)
    return velocity_gradient
```

```python
import functools

import jax
import jax.numpy as jnp
import numpy as np
from jax import lax
from jax.experimental import pallas as pl
from jax.experimental.pallas import tpu as pltpu
from jax.sharding import PartitionSpec as P

COURANT = 0.09
LEAD = 1225.0 / 1024.0
RATIOS = (1.0, -1.0 / 15.0, 1.0 / 125.0, -1.0 / 1715.0)
BAND = 105.0
YOFF = 8


def band_matrices(depth):
    grad = np.zeros((depth, depth), np.float32)
    for i in range(depth):
        for m, ratio in enumerate(RATIOS, start=1):
            if i + m < depth:
                grad[i + m, i] += BAND * ratio
            if i + 1 - m >= 0:
                grad[i + 1 - m, i] -= BAND * ratio
    div = np.zeros((depth, depth), np.float32)
    for i in range(depth):
        for m, ratio in enumerate(RATIOS, start=1):
            if i + m - 1 < depth:
                div[i + m - 1, i] += BAND * ratio
            if i - m >= 0:
                div[i - m, i] -= BAND * ratio
    stack = lambda a: np.concatenate([a, a], axis=0)
    return jnp.asarray(np.stack([stack(grad), stack(div)]), jnp.bfloat16)


def gather_kernel(rows_ref, v_ref, d_ref, *outs):
    owners, _, cap = outs[0].shape[:3]
    for member, out in enumerate(outs):
        def body(dest, carry):
            for j in range(cap):
                row = rows_ref[(member * owners + dest) * cap + j]
                out[dest, 0, j] = v_ref[row]
                out[dest, 1, j] = d_ref[row]
            return carry

        lax.fori_loop(0, owners, body, 0)


def scatter_kernel(rows_ref, *refs):
    arrived, out = refs[:-1], refs[-1]
    out[...] = jnp.zeros_like(out)
    for member, ref in enumerate(arrived):
        sources, cap = ref.shape[:2]

        def body(src, carry):
            for j in range(cap):
                row = rows_ref[(member * sources + src) * cap + j]
                out[row] = out[row] + ref[src, j]
            return carry

        lax.fori_loop(0, sources, body, 0)


def taps(at, low):
    total = None
    for m, ratio in enumerate(RATIOS, start=1):
        up, down = (at(m), at(1 - m)) if low else (at(m - 1), at(-m))
        if up is None and down is None:
            continue
        diff = up - down if up is not None and down is not None else (up if down is None else -down)
        term = diff if m == 1 else ratio * diff
        total = term if total is None else total + term
    return total


def split(value):
    high = value.astype(jnp.bfloat16)
    low = (value - high.astype(jnp.float32)).astype(jnp.bfloat16)
    return jnp.concatenate([high, low], axis=-1)


def shot_kernel(
    slots_ref, source_ref, recv_cells, wave_ref, obs_ref,
    tiles_ref, band_ref, old_ref, now_ref, next_ref, adj_ref,
    out_ref,
    vel, rho, buoy, hx, hy, hz, fy, div_z, pad_u, pad_w, image_one, image_two, third, inject_zero,
):
    nx, ny, nz = now_ref.shape[-3:]
    cap = tiles_ref.shape[2]
    grid_y = ny // 4
    tiles_y = ny // 8
    lane = lax.broadcasted_iota(jnp.int32, (1, nz), 1)
    rows = nx * 8

    def place(kx, carry):
        for ky in range(grid_y):
            slot = slots_ref[kx * grid_y + ky]
            for which, field in ((0, vel), (1, rho)):
                tile = tiles_ref[slot // cap, which, slot % cap].astype(jnp.float32)
                for i in range(4):
                    field[kx * 4 + i, pl.ds(ky * 4, 4), :] = tile[4 * i : 4 * i + 4]
        return carry

    lax.fori_loop(0, nx // 4, place, 0)

    zero_edge = jnp.zeros((nx, YOFF, nz), jnp.float32)
    for ref in (pad_u, pad_w, fy):
        ref[:, pl.ds(0, YOFF), :] = zero_edge
        ref[:, pl.ds(YOFF + ny, YOFF), :] = zero_edge

    def prepare(x, carry):
        value = (0.5 * LEAD * LEAD) / rho[x]
        buoy[x, pl.ds(0, ny), :] = value
        buoy[x, pl.ds(ny, 1), :] = value[ny - 1 :]
        pad_u[x, pl.ds(YOFF, ny), :] = now_ref[0, 0, 0, x].astype(jnp.float32)
        pad_w[x, pl.ds(YOFF, ny), :] = adj_ref[0, 0, 0, x].astype(jnp.float32)
        return carry

    lax.fori_loop(0, nx, prepare, 0, unroll=2)

    def halves(x, carry):
        here = buoy[x, pl.ds(0, ny), :]
        after = buoy[jnp.minimum(x + 1, nx - 1), pl.ds(0, ny), :]
        hx[x] = here + after
        hy[x] = here + buoy[x, pl.ds(1, ny), :]
        shifted = jnp.where(lane == nz - 1, here, pltpu.roll(here, nz - 1, 1))
        hz[x] = (here + shifted) * (1.0 / (BAND * BAND))
        velocity, density = vel[x], rho[x]
        vel[x] = (COURANT * velocity) * (COURANT * velocity) * density
        rho[x] = (2.0 * COURANT * COURANT) * velocity * density
        return carry

    lax.fori_loop(0, nx, halves, 0, unroll=2)

    def operate(field, exact, finish):
        def flux_y(x, carry):
            at = lambda shift: field[x, pl.ds(YOFF + shift, ny), :]
            fy[x, pl.ds(YOFF, ny), :] = hy[x] * taps(at, True)
            return carry

        lax.fori_loop(0, nx, flux_y, 0, unroll=2)

        def tile_loop(ty, carry):
            start = pl.multiple_of(ty * 8, 8)
            here = pl.ds(start, 8)
            padded = pl.ds(pl.multiple_of(start + YOFF, 8), 8)
            block = field[:, padded, :].reshape(rows, nz)
            if exact:
                grad_z = jnp.dot(block.astype(jnp.bfloat16), band_ref[0, :nz], preferred_element_type=jnp.float32)
            else:
                grad_z = jnp.dot(split(block), band_ref[0], preferred_element_type=jnp.float32)
            flux_z = hz[:, here, :].reshape(rows, nz) * grad_z
            div_z[...] = jnp.dot(split(flux_z), band_ref[1], preferred_element_type=jnp.float32).reshape(nx, 8, nz)
            values, fluxes = {}, {}

            def value_at(x):
                if x < 0 or x >= nx:
                    return None
                if x not in values:
                    values[x] = field[x, padded, :]
                return values[x]

            def flux_at(x):
                if x < 0 or x >= nx:
                    return None
                if x not in fluxes:
                    fluxes[x] = hx[x, here, :] * taps(lambda shift: value_at(x + shift), True)
                return fluxes[x]

            for x in range(nx):
                total = taps(lambda shift: flux_at(x + shift), False)
                total = total + taps(lambda shift: fy[x, pl.ds(start + YOFF + shift, 8), :], False)
                total = total + div_z[x]
                finish(x, ty, here, padded, value_at(x), total)
            return carry

        lax.fori_loop(0, tiles_y, tile_loop, 0)

    def add_at(field, offset, cell, amount):
        row, z = cell // nz, cell % nz
        x, y = row // ny, row % ny + offset
        field[x, pl.ds(y, 1), :] += jnp.where(lane == z, amount, 0.0)

    second = pad_w

    def finish_one(x, ty, here, padded, value, total):
        image_one[x, here, :] = total
        third[x, padded, :] = 2.0 * value - old_ref[0, 0, 0, x, here, :].astype(jnp.float32) + vel[x, here, :] * total

    third[:, pl.ds(0, YOFF), :] = zero_edge
    third[:, pl.ds(YOFF + ny, YOFF), :] = zero_edge
    operate(pad_u, True, finish_one)
    add_at(third, YOFF, source_ref[0], wave_ref[0])

    def finish_two(x, ty, here, padded, value, total):
        image_two[x, here, :] = total
        pad_u[x, padded, :] = 2.0 * value - pad_u[x, padded, :] + vel[x, here, :] * total

    operate(third, False, finish_two)
    add_at(pad_u, YOFF, source_ref[0], wave_ref[1])

    q1 = buoy_q1 = inject_zero

    minus_q2 = hz_free = None

    def finish_three(x, ty, here, padded, value, total):
        q1[x, padded, :] = 2.0 * value - next_ref[0, 0, 0, x, here, :].astype(jnp.float32) + vel[x, here, :] * total

    q1[:, pl.ds(0, YOFF), :] = zero_edge
    q1[:, pl.ds(YOFF + ny, YOFF), :] = zero_edge
    operate(second, True, finish_three)

    count = recv_cells.shape[0]

    def receive(step, carry):
        for sub in range(8):
            n = step * 8 + sub
            cell = recv_cells[n]
            row, z = cell // nz, cell % nz
            x, y = row // ny, row % ny + YOFF
            spot = pl.ds(y, 1)
            pick = lane == z
            q1[x, spot, :] += jnp.where(pick, pad_u[x, spot, :] - obs_ref[count + n], 0.0)
            second[x, spot, :] -= jnp.where(pick, third[x, spot, :] - obs_ref[n], 0.0)
        return carry

    lax.fori_loop(0, count // 8, receive, 0)

    def finish_four(x, ty, here, padded, value, total):
        q0 = 2.0 * value - second[x, padded, :] + vel[x, here, :] * total
        result = rho[x, here, :] * (value * image_two[x, here, :] + q0 * image_one[x, here, :])
        for half in range(2):
            slot = slots_ref[(x // 4) * grid_y + ty * 2 + half]
            out_ref[slot // cap, (x % 4) // 2, slot % cap, pl.ds((x % 2) * 4, 4), :] = result[4 * half : 4 * half + 4]

    operate(q1, False, finish_four)


def per_device(
    velocity, density, tile_home, footprints, source_cell, source_wave, receivers, observed,
    pressure_old, pressure_now, adjoint_next, adjoint_now,
):
    owners = lax.axis_size("own")
    cores = lax.axis_size("shot")
    me = lax.axis_index("own")
    my_core = lax.axis_index("shot")
    held = velocity.shape[0]
    members, foot = footprints.shape[2:]
    cap = foot // owners
    nx, ny, nz = pressure_now.shape[-3:]
    home = jnp.take(tile_home, footprints, axis=0)
    slots = jnp.sum((home[..., None, :] < home[..., :, None]).astype(jnp.int32), axis=-1)
    wanted = me * cap + jnp.arange(cap, dtype=jnp.int32)
    row_all = jnp.sum(
        jnp.where(slots[..., None, :] == wanted[:, None], home[..., None, :] - me * held, 0), axis=-1
    )
    row_all = row_all.transpose(2, 0, 1, 3)
    row_mine = lax.dynamic_index_in_dim(row_all, my_core, 2, keepdims=False)
    my_slots = lax.dynamic_index_in_dim(
        lax.dynamic_index_in_dim(slots, me, 0, keepdims=False), my_core, 0, keepdims=False
    )
    vmem = pl.BlockSpec(memory_space=pltpu.VMEM)
    smem = pl.BlockSpec(memory_space=pltpu.SMEM)
    outgoing = pl.pallas_call(
        gather_kernel,
        out_shape=[jax.ShapeDtypeStruct((owners, 2, cap, 16, nz), jnp.bfloat16)] * members,
        in_specs=[smem, vmem, vmem],
        out_specs=[vmem] * members,
    )(row_mine.reshape(-1), velocity.reshape(held, 16, nz), density.reshape(held, 16, nz))
    band = band_matrices(nz)
    plain = pltpu.VMEM((nx, ny, nz), jnp.float32)
    padded = pltpu.VMEM((nx, ny + 2 * YOFF, nz), jnp.float32)
    models = [lax.all_to_all(sent, "own", split_axis=0, concat_axis=0, tiled=True) for sent in outgoing]
    arrived = []
    for member in range(members):
        field = pl.BlockSpec((1, 1, 1, nx, ny, nz), lambda i, member=member: (0, 0, member, 0, 0, 0))
        ready = pl.pallas_call(
            shot_kernel,
            grid=(1,),
            out_shape=jax.ShapeDtypeStruct((owners, cores, cap, 8, nz), jnp.float32),
            in_specs=[smem] * 5 + [vmem, vmem] + [field] * 4,
            out_specs=vmem,
            scratch_shapes=[plain, plain, pltpu.VMEM((nx, ny + 8, nz), jnp.float32), plain, plain, plain, padded,
                            pltpu.VMEM((nx, 8, nz), jnp.float32), padded, padded, plain, plain, padded, padded],
            compiler_params=pltpu.CompilerParams(vmem_limit_bytes=48 * 1024 * 1024),
            cost_estimate=pl.CostEstimate(flops=100_000_000, bytes_accessed=3_000_000, transcendentals=0),
        )(
            my_slots[member],
            source_cell[0, 0, member].reshape(1),
            receivers[0, 0, member],
            source_wave[0, 0, member],
            observed[0, 0, member].reshape(-1),
            models[member], band, pressure_old, pressure_now, adjoint_next, adjoint_now,
        )
        arrived.append(
            lax.all_to_all(
                ready.reshape(owners * cores, cap, 8, nz), ("own", "shot"), split_axis=0, concat_axis=0, tiled=True
            )
        )
    gradient = pl.pallas_call(
        scatter_kernel,
        out_shape=jax.ShapeDtypeStruct((held, 8, nz), jnp.float32),
        in_specs=[smem] + [vmem] * members,
        out_specs=vmem,
    )(row_all.reshape(-1), *arrived)
    return gradient.reshape(held, 4 // cores, 4, nz)


def solution(mesh):
    whole = P(("grp", "own"), None, None, None)
    fields = P(("grp", "own"), "shot", None, None, None, None)
    in_specs = (
        whole, whole, P("grp"), P("grp", None, None, None),
        P(("grp", "own"), "shot", None),
        P(("grp", "own"), "shot", None, None),
        P(("grp", "own"), "shot", None, None),
        P(("grp", "own"), "shot", None, None, None),
        fields, fields, fields, fields,
    )
    return jax.shard_map(
        per_device, mesh=mesh, in_specs=in_specs,
        out_specs=P(("grp", "own"), "shot", None, None), check_vma=False,
    )
```

```python
import functools

import jax
import jax.numpy as jnp
import numpy as np
from jax import lax
from jax.experimental import pallas as pl
from jax.experimental.pallas import tpu as pltpu
from jax.sharding import PartitionSpec as P

COURANT = 0.09
LEAD = 1225.0 / 1024.0
RATIOS = (1.0, -1.0 / 15.0, 1.0 / 125.0, -1.0 / 1715.0)
BAND = 105.0
YOFF = 8


def band_matrices(depth):
    grad = np.zeros((depth, depth), np.float32)
    for i in range(depth):
        for m, ratio in enumerate(RATIOS, start=1):
            if i + m < depth:
                grad[i + m, i] += BAND * ratio
            if i + 1 - m >= 0:
                grad[i + 1 - m, i] -= BAND * ratio
    div = np.zeros((depth, depth), np.float32)
    for i in range(depth):
        for m, ratio in enumerate(RATIOS, start=1):
            if i + m - 1 < depth:
                div[i + m - 1, i] += BAND * ratio
            if i - m >= 0:
                div[i - m, i] -= BAND * ratio
    stack = lambda a: np.concatenate([a, a], axis=0)
    return jnp.asarray(np.stack([stack(grad), stack(div)]), jnp.bfloat16)


def gather_kernel(rows_ref, v_ref, d_ref, *outs):
    owners, _, cap = outs[0].shape[:3]
    for member, out in enumerate(outs):
        def body(dest, carry):
            for j in range(cap):
                row = rows_ref[(member * owners + dest) * cap + j]
                out[dest, 0, j] = v_ref[row]
                out[dest, 1, j] = d_ref[row]
            return carry

        lax.fori_loop(0, owners, body, 0)


def scatter_kernel(rows_ref, *refs):
    arrived, out = refs[:-1], refs[-1]
    out[...] = jnp.zeros_like(out)
    for member, ref in enumerate(arrived):
        sources, cap = ref.shape[:2]

        def body(src, carry):
            for j in range(cap):
                row = rows_ref[(member * sources + src) * cap + j]
                out[row] = out[row] + ref[src, j]
            return carry

        lax.fori_loop(0, sources, body, 0)


def exchange_kernel(axes, sent, got, send_sems, recv_sems, local_sem):
    sizes = [lax.axis_size(axis) for axis in axes]
    peers = sent.shape[0]
    me = lax.axis_index(axes[0])
    for axis, size in zip(axes[1:], sizes[1:]):
        me = me * size + lax.axis_index(axis)

    def place(peer):
        if len(axes) == 1:
            return {axes[0]: peer}
        return {axes[0]: peer // sizes[1], axes[1]: peer % sizes[1]}

    barrier = pltpu.get_barrier_semaphore()

    def greet(d, carry):
        pl.semaphore_signal(barrier, inc=1, device_id=place((me + d) % peers), device_id_type=pl.DeviceIdType.MESH)
        return carry

    lax.fori_loop(1, peers, greet, 0)
    local = pltpu.make_async_copy(sent.at[me], got.at[me], local_sem)
    local.start()
    pl.semaphore_wait(barrier, peers - 1)

    def copy(d):
        peer = (me + d) % peers
        return pltpu.make_async_remote_copy(
            src_ref=sent.at[peer], dst_ref=got.at[me],
            send_sem=send_sems.at[d], recv_sem=recv_sems.at[d],
            device_id=place(peer), device_id_type=pl.DeviceIdType.MESH,
        )

    def start(d, carry):
        copy(d).start()
        return carry

    def wait(d, carry):
        copy(d).wait()
        return carry

    lax.fori_loop(1, peers, start, 0)
    lax.fori_loop(1, peers, wait, 0)
    local.wait()


def exchange(sent, axes, number):
    vmem = pl.BlockSpec(memory_space=pltpu.VMEM)
    return pl.pallas_call(
        functools.partial(exchange_kernel, axes),
        out_shape=jax.ShapeDtypeStruct(sent.shape, sent.dtype),
        in_specs=[vmem], out_specs=vmem,
        scratch_shapes=[pltpu.SemaphoreType.DMA((sent.shape[0],)), pltpu.SemaphoreType.DMA((sent.shape[0],)), pltpu.SemaphoreType.DMA],
        compiler_params=pltpu.CompilerParams(collective_id=number, has_side_effects=True),
    )(sent)


def lookup(tile_home, footprints):
    side = int(round(tile_home.shape[0] ** 0.5))
    foot = int(round(footprints.shape[-1] ** 0.5))
    first = footprints[..., 0].reshape(-1)
    spot = jnp.arange(foot, dtype=jnp.int32)
    along = jnp.arange(side, dtype=jnp.int32)
    pick_x = ((first // side)[:, None] + spot)[..., None] == along
    pick_y = ((first % side)[:, None] + spot)[..., None] == along
    grid = tile_home.reshape(side, side).astype(jnp.float32)
    lines = jnp.dot(pick_x.astype(jnp.float32).reshape(-1, side), grid, precision=lax.Precision.HIGHEST)
    lines = lines.reshape(first.shape[0], foot, 1, side)
    home = jnp.sum(jnp.where(pick_y[:, None], lines, 0.0), axis=-1)
    return home.astype(jnp.int32).reshape(footprints.shape)


def taps(at, low):
    total = None
    for m, ratio in enumerate(RATIOS, start=1):
        up, down = (at(m), at(1 - m)) if low else (at(m - 1), at(-m))
        if up is None and down is None:
            continue
        diff = up - down if up is not None and down is not None else (up if down is None else -down)
        term = diff if m == 1 else ratio * diff
        total = term if total is None else total + term
    return total


def split(value):
    high = value.astype(jnp.bfloat16)
    low = (value - high.astype(jnp.float32)).astype(jnp.bfloat16)
    return jnp.concatenate([high, low], axis=-1)


def shot_kernel(
    slots_ref, source_ref, recv_cells, wave_ref, obs_ref,
    tiles_ref, band_ref, old_ref, now_ref, next_ref, adj_ref,
    out_ref,
    vel, rho, buoy, hx, hy, hz, fy, div_z, pad_u, pad_w, image_one, image_two, third, inject_zero,
):
    nx, ny, nz = now_ref.shape[-3:]
    cap = tiles_ref.shape[2]
    grid_y = ny // 4
    tiles_y = ny // 8
    lane = lax.broadcasted_iota(jnp.int32, (1, nz), 1)
    rows = nx * 8

    def place(kx, carry):
        for ky in range(grid_y):
            slot = slots_ref[kx * grid_y + ky]
            for which, field in ((0, vel), (1, rho)):
                tile = tiles_ref[slot // cap, which, slot % cap].astype(jnp.float32)
                for i in range(4):
                    field[kx * 4 + i, pl.ds(ky * 4, 4), :] = tile[4 * i : 4 * i + 4]
        return carry

    lax.fori_loop(0, nx // 4, place, 0)

    zero_edge = jnp.zeros((nx, YOFF, nz), jnp.float32)
    for ref in (pad_u, pad_w, fy):
        ref[:, pl.ds(0, YOFF), :] = zero_edge
        ref[:, pl.ds(YOFF + ny, YOFF), :] = zero_edge

    def prepare(x, carry):
        value = (0.5 * LEAD * LEAD) / rho[x]
        buoy[x, pl.ds(0, ny), :] = value
        buoy[x, pl.ds(ny, 1), :] = value[ny - 1 :]
        pad_u[x, pl.ds(YOFF, ny), :] = now_ref[0, 0, 0, x].astype(jnp.float32)
        pad_w[x, pl.ds(YOFF, ny), :] = adj_ref[0, 0, 0, x].astype(jnp.float32)
        return carry

    lax.fori_loop(0, nx, prepare, 0, unroll=2)

    def halves(x, carry):
        here = buoy[x, pl.ds(0, ny), :]
        after = buoy[jnp.minimum(x + 1, nx - 1), pl.ds(0, ny), :]
        hx[x] = here + after
        hy[x] = here + buoy[x, pl.ds(1, ny), :]
        shifted = jnp.where(lane == nz - 1, here, pltpu.roll(here, nz - 1, 1))
        hz[x] = (here + shifted) * (1.0 / (BAND * BAND))
        velocity, density = vel[x], rho[x]
        vel[x] = (COURANT * velocity) * (COURANT * velocity) * density
        rho[x] = (2.0 * COURANT * COURANT) * velocity * density
        return carry

    lax.fori_loop(0, nx, halves, 0, unroll=2)

    def operate(field, exact, finish):
        def flux_y(x, carry):
            at = lambda shift: field[x, pl.ds(YOFF + shift, ny), :]
            fy[x, pl.ds(YOFF, ny), :] = hy[x] * taps(at, True)
            return carry

        lax.fori_loop(0, nx, flux_y, 0, unroll=2)

        def tile_loop(ty, carry):
            start = pl.multiple_of(ty * 8, 8)
            here = pl.ds(start, 8)
            padded = pl.ds(pl.multiple_of(start + YOFF, 8), 8)
            block = field[:, padded, :].reshape(rows, nz)
            if exact:
                grad_z = jnp.dot(block.astype(jnp.bfloat16), band_ref[0, :nz], preferred_element_type=jnp.float32)
            else:
                grad_z = jnp.dot(split(block), band_ref[0], preferred_element_type=jnp.float32)
            flux_z = hz[:, here, :].reshape(rows, nz) * grad_z
            div_z[...] = jnp.dot(split(flux_z), band_ref[1], preferred_element_type=jnp.float32).reshape(nx, 8, nz)
            values, fluxes = {}, {}

            def value_at(x):
                if x < 0 or x >= nx:
                    return None
                if x not in values:
                    values[x] = field[x, padded, :]
                return values[x]

            def flux_at(x):
                if x < 0 or x >= nx:
                    return None
                if x not in fluxes:
                    fluxes[x] = hx[x, here, :] * taps(lambda shift: value_at(x + shift), True)
                return fluxes[x]

            for x in range(nx):
                total = taps(lambda shift: flux_at(x + shift), False)
                total = total + taps(lambda shift: fy[x, pl.ds(start + YOFF + shift, 8), :], False)
                total = total + div_z[x]
                finish(x, ty, here, padded, value_at(x), total)
            return carry

        lax.fori_loop(0, tiles_y, tile_loop, 0)

    def add_at(field, offset, cell, amount):
        row, z = cell // nz, cell % nz
        x, y = row // ny, row % ny + offset
        field[x, pl.ds(y, 1), :] += jnp.where(lane == z, amount, 0.0)

    second = pad_w

    def finish_one(x, ty, here, padded, value, total):
        image_one[x, here, :] = total
        third[x, padded, :] = 2.0 * value - old_ref[0, 0, 0, x, here, :].astype(jnp.float32) + vel[x, here, :] * total

    third[:, pl.ds(0, YOFF), :] = zero_edge
    third[:, pl.ds(YOFF + ny, YOFF), :] = zero_edge
    operate(pad_u, True, finish_one)
    add_at(third, YOFF, source_ref[0], wave_ref[0])

    def finish_two(x, ty, here, padded, value, total):
        image_two[x, here, :] = total
        pad_u[x, padded, :] = 2.0 * value - pad_u[x, padded, :] + vel[x, here, :] * total

    operate(third, False, finish_two)
    add_at(pad_u, YOFF, source_ref[0], wave_ref[1])

    q1 = inject_zero

    def finish_three(x, ty, here, padded, value, total):
        q1[x, padded, :] = 2.0 * value - next_ref[0, 0, 0, x, here, :].astype(jnp.float32) + vel[x, here, :] * total

    q1[:, pl.ds(0, YOFF), :] = zero_edge
    q1[:, pl.ds(YOFF + ny, YOFF), :] = zero_edge
    operate(second, True, finish_three)

    count = recv_cells.shape[0]

    def receive(step, carry):
        for sub in range(8):
            n = step * 8 + sub
            cell = recv_cells[n]
            row, z = cell // nz, cell % nz
            x, y = row // ny, row % ny + YOFF
            spot = pl.ds(y, 1)
            pick = lane == z
            q1[x, spot, :] += jnp.where(pick, pad_u[x, spot, :] - obs_ref[count + n], 0.0)
            second[x, spot, :] -= jnp.where(pick, third[x, spot, :] - obs_ref[n], 0.0)
        return carry

    lax.fori_loop(0, count // 8, receive, 0)

    def finish_four(x, ty, here, padded, value, total):
        q0 = 2.0 * value - second[x, padded, :] + vel[x, here, :] * total
        result = rho[x, here, :] * (value * image_two[x, here, :] + q0 * image_one[x, here, :])
        for half in range(2):
            slot = slots_ref[(x // 4) * grid_y + ty * 2 + half]
            out_ref[slot // cap, (x % 4) // 2, slot % cap, pl.ds((x % 2) * 4, 4), :] = result[4 * half : 4 * half + 4]

    operate(q1, False, finish_four)


def per_device(
    velocity, density, tile_home, footprints, source_cell, source_wave, receivers, observed,
    pressure_old, pressure_now, adjoint_next, adjoint_now,
):
    owners = lax.axis_size("own")
    cores = lax.axis_size("shot")
    me = lax.axis_index("own")
    my_core = lax.axis_index("shot")
    held = velocity.shape[0]
    members, foot = footprints.shape[2:]
    cap = foot // owners
    nx, ny, nz = pressure_now.shape[-3:]
    home = lookup(tile_home, footprints)
    slots = jnp.sum((home[..., None, :] < home[..., :, None]).astype(jnp.int32), axis=-1)
    wanted = me * cap + jnp.arange(cap, dtype=jnp.int32)
    row_all = jnp.sum(
        jnp.where(slots[..., None, :] == wanted[:, None], home[..., None, :] - me * held, 0), axis=-1
    )
    row_all = row_all.transpose(2, 0, 1, 3)
    row_mine = lax.dynamic_index_in_dim(row_all, my_core, 2, keepdims=False)
    my_slots = lax.dynamic_index_in_dim(
        lax.dynamic_index_in_dim(slots, me, 0, keepdims=False), my_core, 0, keepdims=False
    )
    vmem = pl.BlockSpec(memory_space=pltpu.VMEM)
    smem = pl.BlockSpec(memory_space=pltpu.SMEM)
    outgoing = pl.pallas_call(
        gather_kernel,
        out_shape=[jax.ShapeDtypeStruct((owners, 2, cap, 16, nz), jnp.bfloat16)] * members,
        in_specs=[smem, vmem, vmem],
        out_specs=[vmem] * members,
    )(row_mine.reshape(-1), velocity.reshape(held, 16, nz), density.reshape(held, 16, nz))
    band = band_matrices(nz)
    plain = pltpu.VMEM((nx, ny, nz), jnp.float32)
    padded = pltpu.VMEM((nx, ny + 2 * YOFF, nz), jnp.float32)
    models = [exchange(outgoing[0], ("own",), 0)]
    for sent in outgoing[1:]:
        sent, models[0] = lax.optimization_barrier((sent, models[0]))
        models.append(lax.all_to_all(sent, "own", split_axis=0, concat_axis=0, tiled=True))
    arrived = []
    for member in range(members):
        field = pl.BlockSpec((1, 1, 1, nx, ny, nz), lambda i, member=member: (0, 0, member, 0, 0, 0))
        ready = pl.pallas_call(
            shot_kernel,
            grid=(1,),
            out_shape=jax.ShapeDtypeStruct((owners, cores, cap, 8, nz), jnp.float32),
            in_specs=[smem] * 5 + [vmem, vmem] + [field] * 4,
            out_specs=vmem,
            scratch_shapes=[plain, plain, pltpu.VMEM((nx, ny + 8, nz), jnp.float32), plain, plain, plain, padded,
                            pltpu.VMEM((nx, 8, nz), jnp.float32), padded, padded, plain, plain, padded, padded],
            compiler_params=pltpu.CompilerParams(vmem_limit_bytes=48 * 1024 * 1024),
            cost_estimate=pl.CostEstimate(flops=100_000_000, bytes_accessed=3_000_000, transcendentals=0),
        )(
            my_slots[member],
            source_cell[0, 0, member].reshape(1),
            receivers[0, 0, member],
            source_wave[0, 0, member],
            observed[0, 0, member].reshape(-1),
            models[member], band, pressure_old, pressure_now, adjoint_next, adjoint_now,
        )
        ready = ready.reshape(owners * cores, cap, 8, nz)
        if member < members - 1:
            arrived.append(lax.all_to_all(ready, ("own", "shot"), split_axis=0, concat_axis=0, tiled=True))
        else:
            arrived.append(exchange(ready, ("own", "shot"), 1))
    gradient = pl.pallas_call(
        scatter_kernel,
        out_shape=jax.ShapeDtypeStruct((held, 8, nz), jnp.float32),
        in_specs=[smem] + [vmem] * members,
        out_specs=vmem,
    )(row_all.reshape(-1), *arrived)
    return gradient.reshape(held, 4 // cores, 4, nz)


def solution(mesh):
    whole = P(("grp", "own"), None, None, None)
    fields = P(("grp", "own"), "shot", None, None, None, None)
    in_specs = (
        whole, whole, P("grp"), P("grp", None, None, None),
        P(("grp", "own"), "shot", None),
        P(("grp", "own"), "shot", None, None),
        P(("grp", "own"), "shot", None, None),
        P(("grp", "own"), "shot", None, None, None),
        fields, fields, fields, fields,
    )
    return jax.shard_map(
        per_device, mesh=mesh, in_specs=in_specs,
        out_specs=P(("grp", "own"), "shot", None, None), check_vma=False,
    )
```

```python
import functools

import jax
import jax.numpy as jnp
import numpy as np
from jax import lax
from jax.experimental import pallas as pl
from jax.experimental.pallas import tpu as pltpu
from jax.sharding import PartitionSpec as P

COURANT = 0.09
LEAD = 1225.0 / 1024.0
RATIOS = (1.0, -1.0 / 15.0, 1.0 / 125.0, -1.0 / 1715.0)
BAND = 105.0
YOFF = 8


def band_matrices(depth):
    grad = np.zeros((depth, depth), np.float32)
    for i in range(depth):
        for m, ratio in enumerate(RATIOS, start=1):
            if i + m < depth:
                grad[i + m, i] += BAND * ratio
            if i + 1 - m >= 0:
                grad[i + 1 - m, i] -= BAND * ratio
    div = np.zeros((depth, depth), np.float32)
    for i in range(depth):
        for m, ratio in enumerate(RATIOS, start=1):
            if i + m - 1 < depth:
                div[i + m - 1, i] += BAND * ratio
            if i - m >= 0:
                div[i - m, i] -= BAND * ratio
    stack = lambda a: np.concatenate([a, a], axis=0)
    return jnp.asarray(np.stack([stack(grad), stack(div)]), jnp.bfloat16)


def gather_kernel(rows_ref, v_ref, d_ref, *outs):
    owners, _, cap = outs[0].shape[:3]
    for member, out in enumerate(outs):
        def body(dest, carry):
            for j in range(cap):
                row = rows_ref[(member * owners + dest) * cap + j]
                out[dest, 0, j] = v_ref[row]
                out[dest, 1, j] = d_ref[row]
            return carry

        lax.fori_loop(0, owners, body, 0)


def scatter_kernel(rows_ref, *refs):
    arrived, out = refs[:-1], refs[-1]
    out[...] = jnp.zeros_like(out)
    for member, ref in enumerate(arrived):
        sources, cap = ref.shape[:2]

        def body(src, carry):
            for j in range(cap):
                row = rows_ref[(member * sources + src) * cap + j]
                out[row] = out[row] + ref[src, j]
            return carry

        lax.fori_loop(0, sources, body, 0)


def exchange_kernel(axes, sent, got, send_sems, recv_sems, local_sem):
    sizes = [lax.axis_size(axis) for axis in axes]
    peers = sent.shape[0]
    me = lax.axis_index(axes[0])
    for axis, size in zip(axes[1:], sizes[1:]):
        me = me * size + lax.axis_index(axis)

    def place(peer):
        if len(axes) == 1:
            return {axes[0]: peer}
        return {axes[0]: peer // sizes[1], axes[1]: peer % sizes[1]}

    barrier = pltpu.get_barrier_semaphore()

    def greet(d, carry):
        pl.semaphore_signal(barrier, inc=1, device_id=place((me + d) % peers), device_id_type=pl.DeviceIdType.MESH)
        return carry

    lax.fori_loop(1, peers, greet, 0)
    local = pltpu.make_async_copy(sent.at[me], got.at[me], local_sem)
    local.start()
    pl.semaphore_wait(barrier, peers - 1)

    def copy(d):
        peer = (me + d) % peers
        return pltpu.make_async_remote_copy(
            src_ref=sent.at[peer], dst_ref=got.at[me],
            send_sem=send_sems.at[d], recv_sem=recv_sems.at[d],
            device_id=place(peer), device_id_type=pl.DeviceIdType.MESH,
        )

    def start(d, carry):
        copy(d).start()
        return carry

    def wait(d, carry):
        copy(d).wait()
        return carry

    lax.fori_loop(1, peers, start, 0)
    lax.fori_loop(1, peers, wait, 0)
    local.wait()


def exchange(sent, axes, number):
    vmem = pl.BlockSpec(memory_space=pltpu.VMEM)
    return pl.pallas_call(
        functools.partial(exchange_kernel, axes),
        out_shape=jax.ShapeDtypeStruct(sent.shape, sent.dtype),
        in_specs=[vmem], out_specs=vmem,
        scratch_shapes=[pltpu.SemaphoreType.DMA((sent.shape[0],)), pltpu.SemaphoreType.DMA((sent.shape[0],)), pltpu.SemaphoreType.DMA],
        compiler_params=pltpu.CompilerParams(collective_id=number, has_side_effects=True),
    )(sent)


def lookup(tile_home, footprints):
    side = int(round(tile_home.shape[0] ** 0.5))
    foot = int(round(footprints.shape[-1] ** 0.5))
    first = footprints[..., 0].reshape(-1)
    spot = jnp.arange(foot, dtype=jnp.int32)
    along = jnp.arange(side, dtype=jnp.int32)
    pick_x = ((first // side)[:, None] + spot)[..., None] == along
    pick_y = ((first % side)[:, None] + spot)[..., None] == along
    grid = tile_home.reshape(side, side).astype(jnp.float32)
    lines = jnp.dot(pick_x.astype(jnp.float32).reshape(-1, side), grid, precision=lax.Precision.HIGHEST)
    lines = lines.reshape(first.shape[0], foot, 1, side)
    home = jnp.sum(jnp.where(pick_y[:, None], lines, 0.0), axis=-1)
    return home.astype(jnp.int32).reshape(footprints.shape)


def taps(at, low):
    total = None
    for m, ratio in enumerate(RATIOS, start=1):
        up, down = (at(m), at(1 - m)) if low else (at(m - 1), at(-m))
        if up is None and down is None:
            continue
        diff = up - down if up is not None and down is not None else (up if down is None else -down)
        term = diff if m == 1 else ratio * diff
        total = term if total is None else total + term
    return total


def split(value):
    high = value.astype(jnp.bfloat16)
    low = (value - high.astype(jnp.float32)).astype(jnp.bfloat16)
    return jnp.concatenate([high, low], axis=-1)


def shot_kernel(
    member, slots_all, source_all, cells_all, wave_all, obs_all,
    tiles_ref, band_ref, old_ref, now_ref, next_ref, adj_ref,
    out_ref,
    vel, rho, buoy, hx, hy, hz, fy, div_z, pad_u, pad_w, image_one, image_two, third, inject_zero,
):
    nx, ny, nz = now_ref.shape[-3:]
    cap = tiles_ref.shape[2]
    grid_y = ny // 4
    tiles_y = ny // 8
    lane = lax.broadcasted_iota(jnp.int32, (1, nz), 1)
    rows = nx * 8

    def place(kx, carry):
        for ky in range(grid_y):
            slot = slots_all[member, kx * grid_y + ky]
            for which, field in ((0, vel), (1, rho)):
                tile = tiles_ref[slot // cap, which, slot % cap].astype(jnp.float32)
                for i in range(4):
                    field[kx * 4 + i, pl.ds(ky * 4, 4), :] = tile[4 * i : 4 * i + 4]
        return carry

    lax.fori_loop(0, nx // 4, place, 0)

    zero_edge = jnp.zeros((nx, YOFF, nz), jnp.float32)
    for ref in (pad_u, pad_w, fy):
        ref[:, pl.ds(0, YOFF), :] = zero_edge
        ref[:, pl.ds(YOFF + ny, YOFF), :] = zero_edge

    def prepare(x, carry):
        value = (0.5 * LEAD * LEAD) / rho[x]
        buoy[x, pl.ds(0, ny), :] = value
        buoy[x, pl.ds(ny, 1), :] = value[ny - 1 :]
        pad_u[x, pl.ds(YOFF, ny), :] = now_ref[0, 0, 0, x].astype(jnp.float32)
        pad_w[x, pl.ds(YOFF, ny), :] = adj_ref[0, 0, 0, x].astype(jnp.float32)
        return carry

    lax.fori_loop(0, nx, prepare, 0, unroll=2)

    def halves(x, carry):
        here = buoy[x, pl.ds(0, ny), :]
        after = buoy[jnp.minimum(x + 1, nx - 1), pl.ds(0, ny), :]
        hx[x] = here + after
        hy[x] = here + buoy[x, pl.ds(1, ny), :]
        shifted = jnp.where(lane == nz - 1, here, pltpu.roll(here, nz - 1, 1))
        hz[x] = (here + shifted) * (1.0 / (BAND * BAND))
        velocity, density = vel[x], rho[x]
        vel[x] = (COURANT * velocity) * (COURANT * velocity) * density
        rho[x] = (2.0 * COURANT * COURANT) * velocity * density
        return carry

    lax.fori_loop(0, nx, halves, 0, unroll=2)

    def operate(field, exact, finish):
        def flux_y(x, carry):
            at = lambda shift: field[x, pl.ds(YOFF + shift, ny), :]
            fy[x, pl.ds(YOFF, ny), :] = hy[x] * taps(at, True)
            return carry

        lax.fori_loop(0, nx, flux_y, 0, unroll=2)

        def tile_loop(ty, carry):
            start = pl.multiple_of(ty * 8, 8)
            here = pl.ds(start, 8)
            padded = pl.ds(pl.multiple_of(start + YOFF, 8), 8)
            block = field[:, padded, :].reshape(rows, nz)
            if exact:
                grad_z = jnp.dot(block.astype(jnp.bfloat16), band_ref[0, :nz], preferred_element_type=jnp.float32)
            else:
                grad_z = jnp.dot(split(block), band_ref[0], preferred_element_type=jnp.float32)
            flux_z = hz[:, here, :].reshape(rows, nz) * grad_z
            div_z[...] = jnp.dot(split(flux_z), band_ref[1], preferred_element_type=jnp.float32).reshape(nx, 8, nz)
            values, fluxes = {}, {}

            def value_at(x):
                if x < 0 or x >= nx:
                    return None
                if x not in values:
                    values[x] = field[x, padded, :]
                return values[x]

            def flux_at(x):
                if x < 0 or x >= nx:
                    return None
                if x not in fluxes:
                    fluxes[x] = hx[x, here, :] * taps(lambda shift: value_at(x + shift), True)
                return fluxes[x]

            for x in range(nx):
                total = taps(lambda shift: flux_at(x + shift), False)
                total = total + taps(lambda shift: fy[x, pl.ds(start + YOFF + shift, 8), :], False)
                total = total + div_z[x]
                finish(x, ty, here, padded, value_at(x), total)
            return carry

        lax.fori_loop(0, tiles_y, tile_loop, 0)

    def add_at(field, offset, cell, amount):
        row, z = cell // nz, cell % nz
        x, y = row // ny, row % ny + offset
        field[x, pl.ds(y, 1), :] += jnp.where(lane == z, amount, 0.0)

    second = pad_w

    def finish_one(x, ty, here, padded, value, total):
        image_one[x, here, :] = total
        third[x, padded, :] = 2.0 * value - old_ref[0, 0, 0, x, here, :].astype(jnp.float32) + vel[x, here, :] * total

    third[:, pl.ds(0, YOFF), :] = zero_edge
    third[:, pl.ds(YOFF + ny, YOFF), :] = zero_edge
    operate(pad_u, True, finish_one)
    add_at(third, YOFF, source_all[0, 0, member], wave_all[0, 0, member, 0])

    def finish_two(x, ty, here, padded, value, total):
        image_two[x, here, :] = total
        pad_u[x, padded, :] = 2.0 * value - pad_u[x, padded, :] + vel[x, here, :] * total

    operate(third, False, finish_two)
    add_at(pad_u, YOFF, source_all[0, 0, member], wave_all[0, 0, member, 1])

    q1 = inject_zero

    def finish_three(x, ty, here, padded, value, total):
        q1[x, padded, :] = 2.0 * value - next_ref[0, 0, 0, x, here, :].astype(jnp.float32) + vel[x, here, :] * total

    q1[:, pl.ds(0, YOFF), :] = zero_edge
    q1[:, pl.ds(YOFF + ny, YOFF), :] = zero_edge
    operate(second, True, finish_three)

    count = cells_all.shape[-1]

    def receive(step, carry):
        for sub in range(8):
            n = step * 8 + sub
            cell = cells_all[0, 0, member, n]
            row, z = cell // nz, cell % nz
            x, y = row // ny, row % ny + YOFF
            spot = pl.ds(y, 1)
            pick = lane == z
            q1[x, spot, :] += jnp.where(pick, pad_u[x, spot, :] - obs_all[0, 0, member, 1, n], 0.0)
            second[x, spot, :] -= jnp.where(pick, third[x, spot, :] - obs_all[0, 0, member, 0, n], 0.0)
        return carry

    lax.fori_loop(0, count // 8, receive, 0)

    def finish_four(x, ty, here, padded, value, total):
        q0 = 2.0 * value - second[x, padded, :] + vel[x, here, :] * total
        result = rho[x, here, :] * (value * image_two[x, here, :] + q0 * image_one[x, here, :])
        for half in range(2):
            slot = slots_all[member, (x // 4) * grid_y + ty * 2 + half]
            out_ref[slot // cap, (x % 4) // 2, slot % cap, pl.ds((x % 2) * 4, 4), :] = result[4 * half : 4 * half + 4]

    operate(q1, False, finish_four)


def per_device(
    velocity, density, tile_home, footprints, source_cell, source_wave, receivers, observed,
    pressure_old, pressure_now, adjoint_next, adjoint_now,
):
    owners = lax.axis_size("own")
    cores = lax.axis_size("shot")
    me = lax.axis_index("own")
    my_core = lax.axis_index("shot")
    held = velocity.shape[0]
    members, foot = footprints.shape[2:]
    cap = foot // owners
    nx, ny, nz = pressure_now.shape[-3:]
    home = lookup(tile_home, footprints)
    slots = jnp.sum((home[..., None, :] < home[..., :, None]).astype(jnp.int32), axis=-1)
    wanted = me * cap + jnp.arange(cap, dtype=jnp.int32)
    row_all = jnp.sum(
        jnp.where(slots[..., None, :] == wanted[:, None], home[..., None, :] - me * held, 0), axis=-1
    )
    row_all = row_all.transpose(2, 0, 1, 3)
    row_mine = lax.dynamic_index_in_dim(row_all, my_core, 2, keepdims=False)
    my_slots = lax.dynamic_index_in_dim(
        lax.dynamic_index_in_dim(slots, me, 0, keepdims=False), my_core, 0, keepdims=False
    )
    vmem = pl.BlockSpec(memory_space=pltpu.VMEM)
    smem = pl.BlockSpec(memory_space=pltpu.SMEM)
    outgoing = pl.pallas_call(
        gather_kernel,
        out_shape=[jax.ShapeDtypeStruct((owners, 2, cap, 16, nz), jnp.bfloat16)] * members,
        in_specs=[smem, vmem, vmem],
        out_specs=[vmem] * members,
    )(row_mine.reshape(-1), velocity.reshape(held, 16, nz), density.reshape(held, 16, nz))
    band = band_matrices(nz)
    plain = pltpu.VMEM((nx, ny, nz), jnp.float32)
    padded = pltpu.VMEM((nx, ny + 2 * YOFF, nz), jnp.float32)
    models = [exchange(outgoing[0], ("own",), 0)]
    for sent in outgoing[1:]:
        sent, models[0] = lax.optimization_barrier((sent, models[0]))
        models.append(lax.all_to_all(sent, "own", split_axis=0, concat_axis=0, tiled=True))
    arrived = []
    for member in range(members):
        field = pl.BlockSpec((1, 1, 1, nx, ny, nz), lambda i, member=member: (0, 0, member, 0, 0, 0))
        ready = pl.pallas_call(
            functools.partial(shot_kernel, member),
            grid=(1,),
            out_shape=jax.ShapeDtypeStruct((owners, cores, cap, 8, nz), jnp.float32),
            in_specs=[smem] * 5 + [vmem, vmem] + [field] * 4,
            out_specs=vmem,
            scratch_shapes=[plain, plain, pltpu.VMEM((nx, ny + 8, nz), jnp.float32), plain, plain, plain, padded,
                            pltpu.VMEM((nx, 8, nz), jnp.float32), padded, padded, plain, plain, padded, padded],
            compiler_params=pltpu.CompilerParams(vmem_limit_bytes=48 * 1024 * 1024),
            cost_estimate=pl.CostEstimate(flops=100_000_000, bytes_accessed=3_000_000, transcendentals=0),
        )(
            my_slots, source_cell, receivers, source_wave, observed,
            models[member], band, pressure_old, pressure_now, adjoint_next, adjoint_now,
        )
        ready = ready.reshape(owners * cores, cap, 8, nz)
        if member < members - 1:
            arrived.append(lax.all_to_all(ready, ("own", "shot"), split_axis=0, concat_axis=0, tiled=True))
        else:
            arrived.append(exchange(ready, ("own", "shot"), 1))
    gradient = pl.pallas_call(
        scatter_kernel,
        out_shape=jax.ShapeDtypeStruct((held, 8, nz), jnp.float32),
        in_specs=[smem] + [vmem] * members,
        out_specs=vmem,
    )(row_all.reshape(-1), *arrived)
    return gradient.reshape(held, 4 // cores, 4, nz)


def solution(mesh):
    whole = P(("grp", "own"), None, None, None)
    fields = P(("grp", "own"), "shot", None, None, None, None)
    in_specs = (
        whole, whole, P("grp"), P("grp", None, None, None),
        P(("grp", "own"), "shot", None),
        P(("grp", "own"), "shot", None, None),
        P(("grp", "own"), "shot", None, None),
        P(("grp", "own"), "shot", None, None, None),
        fields, fields, fields, fields,
    )
    return jax.shard_map(
        per_device, mesh=mesh, in_specs=in_specs,
        out_specs=P(("grp", "own"), "shot", None, None), check_vma=False,
    )
```
